32 devices in a mesh: ctx: 8 (over y, x, core), head: 4 (over z).
Axes of the slice: x: 2, y: 2, z: 4, core: 2. Of those that a mesh axis runs over, the one named last changes fastest.
Arguments:
- tokens: bfloat16 [2, 4096, 1152], P(None, ('ctx', 'head')), may hold values from -6 to 6
- lengths: int32 [2, 4], replicated, may hold values from 1 to 2048, 4096 in all within a row
- attn_in_gain: float32 [1152], replicated, may hold values from 0.25 to 1.75
- query_weight: bfloat16 [1152, 1024], P(None, 'head'), may hold values from -0.1875 to 0.1875
- key_weight: bfloat16 [1152, 256], replicated, may hold values from -0.1875 to 0.1875
- value_weight: bfloat16 [1152, 256], replicated, may hold values from -0.1875 to 0.1875
- query_gain: float32 [256], replicated, may hold values from 0.25 to 1.75
- key_gain: float32 [256], replicated, may hold values from 0.25 to 1.75
- out_weight: bfloat16 [1024, 1152], P('head'), may hold values from -0.1875 to 0.1875
- attn_post_gain: float32 [1152], replicated, may hold values from 0.25 to 1.75
- ffn_in_gain: float32 [1152], replicated, may hold values from 0.25 to 1.75
- gate_up: bfloat16 [1152, 2, 6912], P(None, None, 'head'), may hold values from -0.1875 to 0.1875
- down_weight: bfloat16 [6912, 1152], P('head'), may hold values from -0.078125 to 0.078125
- ffn_out_gain: float32 [1152], replicated, may hold values from 0.25 to 1.75
- cotangent: bfloat16 [2, 4096, 1152], P(None, ('ctx', 'head')), may hold values from -6 to 6
Outputs:
- output: bfloat16 [2, 4096, 1152], P(None, ('ctx', 'head'))
- grad_tokens: float32 [2, 4096, 1152], P(None, ('ctx', 'head'))
- grad_attn_in_gain: float32 [1152], replicated
- grad_query_weight: float32 [1152, 1024], P(None, 'head')
- grad_key_weight: float32 [1152, 256], replicated
- grad_value_weight: float32 [1152, 256], replicated
- grad_query_gain: float32 [256], replicated
- grad_key_gain: float32 [256], replicated
- grad_out_weight: float32 [1024, 1152], P('head')
- grad_attn_post_gain: float32 [1152], replicated
- grad_ffn_in_gain: float32 [1152], replicated
- grad_gate_up: float32 [1152, 2, 6912], P(None, None, 'head')
- grad_down_weight: float32 [6912, 1152], P('head')
- grad_ffn_out_gain: float32 [1152], replicated
The draws below stay inside these ranges and needn't reach their ends.
Inputs may be any that keep to these rules, and one draw needn't show every extreme that they name: Each row holds the lengths of 4 sequences packed back to back that fill all 4096 tokens; the longest is exactly 2048.
All inputs are finite; a program needn't handle non-finite values.
Results may differ from the reference program's by a relative error of at most 0.02.
Values may be sent and summed in bfloat16 or wider, within the bound.
A program may use at most 320 MiB of HBM per device.

```python
import math
import jax
import jax.numpy as jnp
import numpy as np
from jax import lax

D = 1152
HEADS = 4
HD = 256
FF = 6912
MICRO = 2
SEQS = 4
QROWS = 512
TOKENS = 4096
MOST_LEN = 2048


def shard_levels(stream_key, dims, cuts, low, high):
    factor_of, own = 1.0, jax.random.fold_in(stream_key, 6)
    for position, shards_of in cuts:
        heights = jnp.exp(jax.random.uniform(jax.random.fold_in(own, position), (shards_of,), jnp.float32, low / len(cuts), high / len(cuts)))
        factor_of = factor_of * jnp.repeat(heights, dims[position] // shards_of).reshape([-1 if axis == position else 1 for axis in range(len(dims))])
    return factor_of


def length_profile(number_of, total, bound, slope):
    portions = [(1 << 20) // math.isqrt(rank ** slope) + 1 for rank in range(2, number_of + 1)]
    surplus, given = total - bound - (number_of - 1), [1] * (number_of - 1)
    while surplus > 0:
        free = [i for i in range(number_of - 1) if given[i] < bound]
        pool, budget = sum([portions[i] for i in free]), surplus
        for i in free:
            extra = min(bound - given[i], max(1, budget * portions[i] // pool), surplus)
            given[i] = given[i] + extra
            surplus = surplus - extra
    return np.array([bound] + given)


def uneven_parts(stream_key, count, total, limit, skew):
    if count == 2:
        one = jax.random.randint(stream_key, (), max(1, total - limit), min(limit, total - 1) + 1)
        return jnp.stack([one, total - one])
    sizes = jnp.asarray(length_profile(count, total, limit, skew), jnp.int32)
    twos = (count - 1) // 2
    source_of, sink = sizes[1:1 + 2 * twos:2], sizes[2:2 + 2 * twos:2]
    room = jnp.minimum(source_of - 1, limit - sink)
    shifted = jax.random.randint(jax.random.fold_in(stream_key, 1), (twos,), 0, 1 << 20) % (room + 1)
    sizes = sizes.at[1:1 + 2 * twos:2].set(source_of - shifted).at[2:2 + 2 * twos:2].set(sink + shifted)
    return sizes[jax.random.permutation(jax.random.fold_in(stream_key, 2), count)]


def bell_draw(stream_key, shape, spread, limit, cuts=(), held_as=jnp.bfloat16):
    result = jax.random.normal(stream_key, shape, jnp.float32) * spread
    if len(cuts) > 0:
        result = shard_levels(stream_key, shape, cuts, -0.22, 0.18) * result
    return jnp.clip(result, min=-limit, max=limit).astype(held_as)


def setup_inputs(seed: int = 0) -> dict:
    key_of = jax.random.split(jax.random.key(seed), 16)
    return {
        "tokens": bell_draw(key_of[0], (MICRO, TOKENS, D), 1.0, 6.0, ((1, 32),)),
        "lengths": jax.vmap(lambda own: uneven_parts(own, SEQS, TOKENS, MOST_LEN, 2))(jax.random.split(key_of[1], MICRO)).reshape((MICRO, SEQS)).astype(jnp.int32),
        "attn_in_gain": jnp.clip(1.0 + 0.15 * jax.random.normal(key_of[2], (D,), jnp.float32), 0.25, 1.75),
        "query_weight": bell_draw(key_of[3], (D, HEADS * HD), D ** -0.5, 0.1875, ((1, 4),)),
        "key_weight": bell_draw(key_of[4], (D, HD), D ** -0.5, 0.1875),
        "value_weight": bell_draw(key_of[5], (D, HD), D ** -0.5, 0.1875),
        "query_gain": jnp.clip(1.0 + 0.15 * jax.random.normal(key_of[6], (HD,), jnp.float32), 0.25, 1.75),
        "key_gain": jnp.clip(1.0 + 0.15 * jax.random.normal(key_of[7], (HD,), jnp.float32), 0.25, 1.75),
        "out_weight": bell_draw(key_of[8], (HEADS * HD, D), (HEADS * HD) ** -0.5, 0.1875, ((0, 4),)),
        "attn_post_gain": jnp.clip(1.0 + 0.15 * jax.random.normal(key_of[9], (D,), jnp.float32), 0.25, 1.75),
        "ffn_in_gain": jnp.clip(1.0 + 0.15 * jax.random.normal(key_of[10], (D,), jnp.float32), 0.25, 1.75),
        "gate_up": bell_draw(key_of[11], (D, 2, FF), D ** -0.5, 0.1875, ((2, 4),)),
        "down_weight": bell_draw(key_of[12], (FF, D), FF ** -0.5, 0.078125, ((0, 4),)),
        "ffn_out_gain": jnp.clip(1.0 + 0.15 * jax.random.normal(key_of[13], (D,), jnp.float32), 0.25, 1.75),
        "cotangent": bell_draw(key_of[14], (MICRO, TOKENS, D), 1.0, 6.0, ((1, 32),)),
    }


@jax.custom_vjp
def low(v):
    return lax.optimization_barrier(v.astype(jnp.bfloat16)).astype(jnp.float32)

@jax.custom_vjp
def low_back(v):
    return v

def low_keep(v):
    return (low(v), None)

def low_pass(kept, grad):
    return (grad,)

def back_keep(v):
    return (v, None)

def back_low(kept, grad):
    return (low(grad),)
low.defvjp(low_keep, low_pass)
low_back.defvjp(back_keep, back_low)
EPS = 1e-06
THETA = 1000000.0
NEGATIVE = -1e+30

def matmul(left, right):
    return jnp.dot(left, right, precision=lax.Precision.HIGHEST, preferred_element_type=jnp.float32)

def rms_norm(field_in, gain_vec):
    return field_in * lax.rsqrt(lax.optimization_barrier(jnp.mean(field_in * field_in, axis=-1, keepdims=True)) + EPS) * gain_vec

def rotate(field_in, cosine, sine_table):
    half_width = field_in.shape[-1] // 2
    first_half = field_in[:, :half_width]
    second_half = field_in[:, half_width:]
    return jnp.concatenate([first_half * cosine - second_half * sine_table, second_half * cosine + first_half * sine_table], axis=1)

def prepare(field_in, gain_vec, cosine, sine_table):
    return rotate(rms_norm(field_in, gain_vec), cosine, sine_table)

def gated_gelu(gate_val, up_val):
    return jax.nn.gelu(gate_val, approximate=True) * up_val

def row_starts(lengths_row, token_index):
    seq_ends = jnp.cumsum(lengths_row, dtype=jnp.int32)
    passed = (token_index[:, None] >= seq_ends[None, :]).astype(jnp.int32)
    return lax.optimization_barrier(jnp.sum(passed * lengths_row[None, :], axis=1, dtype=jnp.int32)).astype(jnp.int32)

def angles(positions, width):
    half_width = width // 2
    frequency = jnp.power(THETA, -(jnp.arange(half_width, dtype=jnp.float32) * 2.0 / width))
    phase_angle = positions.astype(jnp.float32)[:, None] * frequency[None, :]
    return (jnp.cos(phase_angle), jnp.sin(phase_angle))

def attention(queries, key_rows, values, token_index, starts):
    score_scale = HD ** (-0.5)

    def one_block(blocks):
        block_queries, block_index, block_start = blocks
        scores = low_back(matmul(block_queries, key_rows.T) * score_scale)
        allowed = (token_index[None, :] <= block_index[:, None]) & (token_index[None, :] >= block_start[:, None])
        scores = jnp.where(allowed, scores, NEGATIVE)
        row_top = lax.optimization_barrier(jnp.max(scores, axis=1, keepdims=True))
        weights = jnp.exp(scores - row_top)
        probs = low(weights / lax.optimization_barrier(jnp.sum(weights, axis=1, keepdims=True)))
        return matmul(probs, values)
    block_count = TOKENS // QROWS
    blocks = (queries.reshape(block_count, QROWS, HD), token_index.reshape(block_count, QROWS), starts.reshape(block_count, QROWS))
    return lax.map(jax.checkpoint(one_block), blocks).reshape(TOKENS, HD)

def block_layer(inputs, lengths_row, params):
    attn_in_gain, query_weight, key_weight, value_weight, query_gain, key_gain, out_weight, attn_post_gain, ffn_in_gain, gate_up, down_weight, ffn_out_gain = params
    token_index = jnp.arange(TOKENS, dtype=jnp.int32)
    starts = row_starts(lengths_row, token_index)
    cosine, sine_table = angles(token_index - starts, HD)
    normed_one = low(rms_norm(inputs, attn_in_gain))
    query_all = low_back(matmul(normed_one, query_weight))
    key_pre = matmul(normed_one, key_weight)
    value_pre = matmul(normed_one, value_weight)
    head_outputs = []
    for head_id in range(HEADS):
        queries = low(prepare(query_all[:, head_id * HD:(head_id + 1) * HD], query_gain, cosine, sine_table))
        key_rows = low(prepare(low_back(key_pre), key_gain, cosine, sine_table))
        values = low(low_back(value_pre))
        head_outputs.append(low(low_back(attention(queries, key_rows, values, token_index, starts))))
    mixed = low_back(matmul(jnp.concatenate(head_outputs, axis=1), out_weight))
    middle = inputs + rms_norm(mixed, attn_post_gain)
    normed_two = low(rms_norm(middle, ffn_in_gain))
    gate_val = low_back(matmul(normed_two, gate_up[:, 0, :]))
    up_val = low_back(matmul(normed_two, gate_up[:, 1, :]))
    hidden = low(gated_gelu(gate_val, up_val))
    branch = low_back(matmul(hidden, down_weight))
    return middle + rms_norm(branch, ffn_out_gain)

def reference(tokens, lengths, attn_in_gain, query_weight, key_weight, value_weight, query_gain, key_gain, out_weight, attn_post_gain, ffn_in_gain, gate_up, down_weight, ffn_out_gain, cotangent):
    params = (attn_in_gain.astype(jnp.float32), query_weight.astype(jnp.float32), key_weight.astype(jnp.float32), value_weight.astype(jnp.float32), query_gain.astype(jnp.float32), key_gain.astype(jnp.float32), out_weight.astype(jnp.float32), attn_post_gain.astype(jnp.float32), ffn_in_gain.astype(jnp.float32), gate_up.astype(jnp.float32), down_weight.astype(jnp.float32), ffn_out_gain.astype(jnp.float32))
    inputs = tokens.astype(jnp.float32)

    def forward(inputs, params):
        return jnp.stack([block_layer(inputs[batch_index], lengths[batch_index], params) for batch_index in range(MICRO)])
    output, pullback = jax.vjp(forward, inputs, params)
    grad_tokens, grads = pullback(cotangent.astype(jnp.float32))
    grad_attn_in_gain, grad_query_weight, grad_key_weight, grad_value_weight, grad_query_gain, grad_key_gain, grad_out_weight, grad_attn_post_gain, grad_ffn_in_gain, grad_gate_up, grad_down_weight, grad_ffn_out_gain = grads
    return (output.astype(jnp.bfloat16), grad_tokens, grad_attn_in_gain, grad_query_weight, grad_key_weight, grad_value_weight, grad_query_gain, grad_key_gain, grad_out_weight, grad_attn_post_gain, grad_ffn_in_gain, grad_gate_up, grad_down_weight, grad_ffn_out_gain)
```

```python
from functools import partial

import jax
import jax.numpy as jnp
from jax import lax
from jax.experimental import pallas as pl
from jax.experimental.pallas import tpu as pltpu
from jax.sharding import PartitionSpec as P

EPS = 1e-06
THETA = 1000000.0
NEGATIVE = -1e30
AXES = ("ctx", "head")
BF = jnp.bfloat16
F32 = jnp.float32


def rms_norm(field_in, gain_vec):
    return (
        field_in * lax.rsqrt(jnp.mean(field_in * field_in, axis=-1, keepdims=True) + EPS) * gain_vec
    )


def rotate(field_in, cosine, sine_table):
    half_width = field_in.shape[-1] // 2
    first_half = field_in[..., :half_width]
    second_half = field_in[..., half_width:]
    return jnp.concatenate(
        [
            first_half * cosine - second_half * sine_table,
            second_half * cosine + first_half * sine_table,
        ],
        axis=-1,
    )


def prepare(field_in, gain_vec, cosine, sine_table):
    return rotate(rms_norm(field_in, gain_vec), cosine, sine_table)


def gated_gelu(gate_val, up_val):
    return jax.nn.gelu(gate_val, approximate=True) * up_val


def row_starts(lengths_row, token_index):
    seq_ends = jnp.cumsum(lengths_row, dtype=jnp.int32)
    passed = (token_index[:, None] >= seq_ends[None, :]).astype(jnp.int32)
    return jnp.sum(passed * lengths_row[None, :], axis=1, dtype=jnp.int32)


def angles(positions, width):
    half_width = width // 2
    frequency = jnp.power(THETA, -(jnp.arange(half_width, dtype=F32) * 2.0 / width))
    phase_angle = positions.astype(F32)[:, None] * frequency[None, :]
    return (jnp.cos(phase_angle), jnp.sin(phase_angle))


def mm(left, right):
    return jnp.dot(left, right, preferred_element_type=F32)


def mm_nt(left, right):
    return lax.dot_general(left, right, (((1,), (1,)), ((), ())), preferred_element_type=F32)


def mm_tn(left, right):
    return lax.dot_general(left, right, (((0,), (0,)), ((), ())), preferred_element_type=F32)


def block_scalars(meta, seqs, query_ctx, z, z_count, rows):
    first_query = (query_ctx * z_count + z) * rows
    start = jnp.int32(0)
    end = jnp.int32(0)
    for s in range(seqs):
        end = end + meta[s]
        start = jnp.where(first_query >= end, end, start)
    return first_query, start


def scores_of(meta, seqs, q, kv, first_query, first_key, z, rows, head_dim):
    stacked = q.shape[0]
    keys = kv.shape[0]
    scores = mm_nt(q, kv[:, :head_dim]) * (head_dim**-0.5)
    key_row = lax.broadcasted_iota(jnp.int32, (1, keys), 1)
    key_index = first_key + ((key_row // rows) ^ z) * rows + key_row % rows
    query_index = first_query + lax.broadcasted_iota(jnp.int32, (stacked, 1), 0) % rows
    start = jnp.zeros((stacked, 1), jnp.int32)
    end = jnp.int32(0)
    for s in range(seqs):
        end = end + meta[s]
        start = jnp.where(query_index >= end, end, start)
    allowed = (key_index <= query_index) & (key_index >= start)
    return scores, allowed


def forward_kernel(seqs, rows, z_count, meta, q_ref, kv_ref, o_ref, lse_ref, top, total):
    step = pl.program_id(0)
    last = pl.num_programs(0) - 1
    pair, z = meta[seqs], meta[seqs + 1]
    head_dim = q_ref.shape[-1]
    key_ctx = 2 * ((step // 2) ^ pair) + step % 2
    first_key = key_ctx * z_count * rows

    @pl.when(step == 0)
    def _():
        top[...] = jnp.full(top.shape, NEGATIVE, F32)
        total[...] = jnp.zeros(total.shape, F32)
        o_ref[...] = jnp.zeros(o_ref.shape, F32)

    for block in range(2):
        first_query, first_start = block_scalars(meta, seqs, 2 * pair + block, z, z_count, rows)
        needed = (first_key < first_query + rows) & (first_key + z_count * rows > first_start)

        @pl.when(needed)
        def _():
            kv = kv_ref[0]
            scores, allowed = scores_of(
                meta, seqs, q_ref[block], kv, first_query, first_key, z, rows, head_dim
            )
            scores = jnp.where(allowed, scores, NEGATIVE)
            old_top = top[block][:, :1]
            new_top = jnp.maximum(old_top, jnp.max(scores, axis=1, keepdims=True))
            weights = jnp.where(allowed, jnp.exp(scores - new_top), 0.0)
            keep = jnp.exp(old_top - new_top)
            new_total = total[block][:, :1] * keep + jnp.sum(weights, axis=1, keepdims=True)
            o_ref[block] = o_ref[block] * keep + mm(weights.astype(BF), kv[:, head_dim:])
            top[block] = jnp.broadcast_to(new_top, top.shape[1:])
            total[block] = jnp.broadcast_to(new_total, total.shape[1:])

    @pl.when(step == last)
    def _():
        for block in range(2):
            o_ref[block] = o_ref[block] / total[block][:, :1]
            lse_ref[block] = top[block] + jnp.log(total[block])


def backward_kernel(
    seqs, rows, z_count, meta, q_ref, do_ref, o_ref, lse_ref, kv_ref, dq_ref, dkv_ref, delta, acc
):
    step = pl.program_id(0)
    pair, z = meta[seqs], meta[seqs + 1]
    head_dim = q_ref.shape[-1]
    scale = head_dim**-0.5
    key_ctx = 2 * ((step // 2) ^ pair) + step % 2
    first_key = key_ctx * z_count * rows

    @pl.when(step == 0)
    def _():
        dq_ref[...] = jnp.zeros(dq_ref.shape, F32)
        for block in range(2):
            delta[block] = jnp.broadcast_to(
                jnp.sum(o_ref[block] * do_ref[block].astype(F32), axis=1, keepdims=True),
                delta.shape[1:],
            )

    acc[...] = jnp.zeros(acc.shape, F32)
    for block in range(2):
        first_query, first_start = block_scalars(meta, seqs, 2 * pair + block, z, z_count, rows)
        needed = (first_key < first_query + rows) & (first_key + z_count * rows > first_start)

        @pl.when(needed)
        def _():
            kv = kv_ref[0]
            q = q_ref[block]
            d_out = do_ref[block]
            scores, allowed = scores_of(
                meta, seqs, q, kv, first_query, first_key, z, rows, head_dim
            )
            weights = jnp.where(allowed, jnp.exp(scores - lse_ref[block][:, :1]), 0.0)
            d_weights = mm_nt(d_out, kv[:, head_dim:])
            d_scores = (weights * (d_weights - delta[block][:, :1])).astype(BF)
            acc[:, head_dim:] += mm_tn(weights.astype(BF), d_out)
            acc[:, :head_dim] += mm_tn(d_scores, q) * scale
            dq_ref[block] += mm(d_scores, kv[:, :head_dim]) * scale

    dkv_ref[0] = acc[...].astype(BF)


def attend(meta, seqs, rows, z_count, q, kv):
    ctx_count, keys, wide = kv.shape
    _, stacked, head_dim = q.shape
    whole = lambda *shape: pl.BlockSpec(shape, lambda i, m: (0,) * len(shape))
    return pl.pallas_call(
        partial(forward_kernel, seqs, rows, z_count),
        out_shape=(
            jax.ShapeDtypeStruct((2, stacked, head_dim), F32),
            jax.ShapeDtypeStruct((2, stacked, 128), F32),
        ),
        grid_spec=pltpu.PrefetchScalarGridSpec(
            num_scalar_prefetch=1,
            grid=(ctx_count,),
            in_specs=[
                whole(2, stacked, head_dim),
                pl.BlockSpec((1, keys, wide), lambda i, m: (i, 0, 0)),
            ],
            out_specs=(whole(2, stacked, head_dim), whole(2, stacked, 128)),
            scratch_shapes=[pltpu.VMEM((2, stacked, 128), F32)] * 2,
        ),
        compiler_params=pltpu.CompilerParams(
            dimension_semantics=("arbitrary",), vmem_limit_bytes=48 * 2**20
        ),
        name="attend",
    )(meta, q, kv)


def attend_back(meta, seqs, rows, z_count, q, d_out, o, lse, kv):
    ctx_count, keys, wide = kv.shape
    _, stacked, head_dim = q.shape
    whole = lambda *shape: pl.BlockSpec(shape, lambda i, m: (0,) * len(shape))
    return pl.pallas_call(
        partial(backward_kernel, seqs, rows, z_count),
        out_shape=(
            jax.ShapeDtypeStruct((2, stacked, head_dim), F32),
            jax.ShapeDtypeStruct(kv.shape, BF),
        ),
        grid_spec=pltpu.PrefetchScalarGridSpec(
            num_scalar_prefetch=1,
            grid=(ctx_count,),
            in_specs=[
                whole(2, stacked, head_dim),
                whole(2, stacked, head_dim),
                whole(2, stacked, head_dim),
                whole(2, stacked, 128),
                pl.BlockSpec((1, keys, wide), lambda i, m: (i, 0, 0)),
            ],
            out_specs=(
                whole(2, stacked, head_dim),
                pl.BlockSpec((1, keys, wide), lambda i, m: (i, 0, 0)),
            ),
            scratch_shapes=[pltpu.VMEM((2, stacked, 128), F32), pltpu.VMEM((keys, wide), F32)],
        ),
        compiler_params=pltpu.CompilerParams(
            dimension_semantics=("arbitrary",), vmem_limit_bytes=48 * 2**20
        ),
        name="attend_back",
    )(meta, q, d_out, o, lse, kv)


class Exchange:
    def __init__(self, ctx_count, z_count):
        self.ctx_count, self.z_count = ctx_count, z_count
        self.pair_bits = [1 << b for b in range(1, ctx_count.bit_length() - 1)]

    def flip(self, value, ctx_bits, z_bits):
        pairs = [
            (c * self.z_count + z, (c ^ ctx_bits) * self.z_count + (z ^ z_bits))
            for c in range(self.ctx_count)
            for z in range(self.z_count)
        ]
        return lax.ppermute(value, AXES, pairs)

    def core(self, value):
        return self.flip(value, 1, 0)

    def gather(self, even, odd):
        both = jnp.stack([even, odd])
        columns = [both] + [self.flip(both, 0, d) for d in range(1, self.z_count)]
        slots = [[[None] * self.z_count for _ in range(2)] for _ in range(self.ctx_count // 2)]
        for d, column in enumerate(columns):
            for parity, bits in ((0, self.pair_bits), (1, self.pair_bits[::-1])):
                have = {0: column[parity]}
                for bit in bits:
                    order = sorted(have)
                    got = self.flip(jnp.stack([have[s] for s in order]), bit, 0)
                    for position, slot in enumerate(order):
                        have[slot | (bit >> 1)] = got[position]
                for slot, value in have.items():
                    slots[slot][parity][d] = value
        return jnp.stack(
            [jnp.concatenate(line, axis=0) for slot in slots for line in slot], axis=0
        )

    def scatter_sum(self, parts):
        totals = []
        for d in range(self.z_count):
            both = []
            for parity, bits in ((0, self.pair_bits[::-1]), (1, self.pair_bits)):
                have = {s: parts[s, parity, d] for s in range(self.ctx_count // 2)}
                for bit in bits:
                    away = sorted(s for s in have if s & (bit >> 1))
                    got = self.flip(jnp.stack([have[s].astype(BF) for s in away]), bit, 0)
                    for position, slot in enumerate(away):
                        home = slot ^ (bit >> 1)
                        have[home] = have[home].astype(F32) + got[position].astype(F32)
                        del have[slot]
                both.append(have[0])
            both = jnp.stack(both)
            totals.append(both if d == 0 else self.flip(both.astype(BF), 0, d))
        return sum(t.astype(F32) for t in totals)

    def swap(self, value, parity):
        mine = jnp.where(parity == 0, value[0], value[1])
        other = self.core(jnp.where(parity == 0, value[1], value[0]))
        return jnp.where(parity == 0, mine, other), jnp.where(parity == 0, other, mine)


def body(
    tokens,
    lengths,
    attn_in_gain,
    query_weight,
    key_weight,
    value_weight,
    query_gain,
    key_gain,
    out_weight,
    attn_post_gain,
    ffn_in_gain,
    gate_up,
    down_weight,
    ffn_out_gain,
    cotangent,
):
    micro, rows, width = tokens.shape
    seqs = lengths.shape[1]
    head_dim = query_weight.shape[1]
    ffn_local = down_weight.shape[0]
    ctx_count, heads = lax.axis_size("ctx"), lax.axis_size("head")
    ctx, z = lax.axis_index("ctx"), lax.axis_index("head")
    parity, pair = ctx % 2, ctx // 2
    net = Exchange(ctx_count, heads)
    all_rows = micro * rows

    all_query = lax.all_gather(query_weight, "head", axis=0)
    all_out = lax.all_gather(out_weight, "head", axis=0)
    gate_weight, up_weight = gate_up[:, 0, :], gate_up[:, 1, :]
    kv_weight = jnp.concatenate([key_weight, value_weight], axis=1)

    query_index = (ctx * heads + z) * rows + jnp.arange(rows, dtype=jnp.int32)
    tables = [
        angles(query_index - row_starts(lengths[b], query_index), head_dim) for b in range(micro)
    ]
    cosine = jnp.concatenate([t[0] for t in tables])
    sine_table = jnp.concatenate([t[1] for t in tables])
    meta = jnp.concatenate(
        [
            jnp.where(parity == 0, lengths[0], lengths[1]).astype(jnp.int32),
            jnp.stack([pair, z]).astype(jnp.int32),
        ]
    )

    inputs = tokens.astype(F32).reshape(all_rows, width)
    normed_f, in_pull = jax.vjp(rms_norm, inputs, attn_in_gain)
    normed_one = normed_f.astype(BF)
    kv_pre = mm(normed_one, kv_weight)
    key_f, key_pull = jax.vjp(
        partial(prepare, cosine=cosine, sine_table=sine_table), kv_pre[:, :head_dim], key_gain
    )
    own_kv = jnp.concatenate([key_f.astype(BF), kv_pre[:, head_dim:].astype(BF)], axis=1)
    even_kv, odd_kv = net.swap(own_kv.reshape(micro, rows, 2 * head_dim), parity)
    kv_slots = net.gather(even_kv, odd_kv)

    query_pre = lax.dot_general(
        normed_one, all_query, (((1,), (1,)), ((), ())), preferred_element_type=F32
    )
    query_pre = jnp.swapaxes(query_pre, 0, 1)
    query_f, query_pull = jax.vjp(
        partial(prepare, cosine=cosine[None], sine_table=sine_table[None]), query_pre, query_gain
    )

    def to_pair(value):
        by_micro = jnp.swapaxes(value.reshape(heads, micro, rows, head_dim), 0, 1)
        even, odd = net.swap(by_micro, parity)
        return jnp.stack([even, odd]).reshape(2, heads * rows, head_dim)

    def from_pair(value):
        first, second = net.swap(value.reshape(2, heads, rows, head_dim), parity)
        return jnp.concatenate([first, second], axis=1)

    queries = to_pair(query_f.astype(BF))
    attended_f, lse = attend(meta, seqs, rows, heads, queries, kv_slots)
    attended = from_pair(attended_f.astype(BF))
    mixed = lax.dot_general(
        jnp.swapaxes(attended, 0, 1).reshape(all_rows, heads * head_dim),
        all_out.reshape(heads * head_dim, width),
        (((1,), (0,)), ((), ())),
        preferred_element_type=F32,
    )
    post_f, post_pull = jax.vjp(rms_norm, mixed, attn_post_gain)
    middle = inputs + post_f
    pre_f, pre_pull = jax.vjp(rms_norm, middle, ffn_in_gain)
    rows_two = [pre_f.astype(BF)]
    rows_two += [net.flip(rows_two[0], 0, d) for d in range(1, heads)]

    branch_parts, hiddens, gelu_pulls = [], [], []
    for d in range(heads):
        hidden_f, gelu_pull = jax.vjp(
            gated_gelu, mm(rows_two[d], gate_weight), mm(rows_two[d], up_weight)
        )
        hiddens.append(hidden_f.astype(BF))
        gelu_pulls.append(gelu_pull)
        part = mm(hiddens[d], down_weight)
        branch_parts.append(part if d == 0 else net.flip(part.astype(BF), 0, d))
    branch = sum(p.astype(F32) for p in branch_parts)
    out_f, out_pull = jax.vjp(rms_norm, branch, ffn_out_gain)
    output = (middle + out_f).astype(BF)

    upstream = cotangent.astype(F32).reshape(all_rows, width)
    d_branch, d_out_gain = out_pull(upstream)
    rows_grad = [d_branch.astype(BF)]
    rows_grad += [net.flip(rows_grad[0], 0, d) for d in range(1, heads)]
    d_gates, d_ups, d_parts = [], [], []
    for d in range(heads):
        d_gate, d_up = gelu_pulls[d](mm_nt(rows_grad[d], down_weight))
        d_gates.append(d_gate.astype(BF))
        d_ups.append(d_up.astype(BF))
        part = mm_nt(d_gates[d], gate_weight) + mm_nt(d_ups[d], up_weight)
        d_parts.append(part if d == 0 else net.flip(part.astype(BF), 0, d))
    d_normed_two = sum(p.astype(F32) for p in d_parts)
    grad_down = mm_tn(jnp.concatenate(hiddens), jnp.concatenate(rows_grad))
    grad_down = lax.psum(grad_down.astype(BF), "ctx")
    rows_all = jnp.concatenate(rows_two)
    grad_gate = mm_tn(rows_all, jnp.concatenate(d_gates))
    grad_up = mm_tn(rows_all, jnp.concatenate(d_ups))
    grad_gate, grad_up = lax.psum((grad_gate.astype(BF), grad_up.astype(BF)), "ctx")

    d_middle, d_ffn_gain = pre_pull(d_normed_two)
    d_middle = d_middle + upstream
    d_mixed, d_post_gain = post_pull(d_middle)
    d_mixed = d_mixed.astype(BF)
    grad_out = jnp.einsum("hrk,rd->hkd", attended, d_mixed, preferred_element_type=F32)
    d_attended = jnp.einsum("rd,hkd->hrk", d_mixed, all_out, preferred_element_type=F32)
    d_attended = to_pair(d_attended.astype(BF))
    d_queries, d_kv_slots = attend_back(
        meta, seqs, rows, heads, queries, d_attended, attended_f, lse, kv_slots
    )
    d_even, d_odd = net.scatter_sum(
        d_kv_slots.reshape(ctx_count // 2, 2, heads, rows, 2 * head_dim)
    )
    first, second = net.swap(jnp.stack([d_even, d_odd]), parity)
    d_kv = jnp.concatenate([first, second])
    d_query_pre, d_query_gain = query_pull(from_pair(d_queries))
    d_key_pre, d_key_gain = key_pull(d_kv[:, :head_dim])
    d_query_pre = d_query_pre.astype(BF)
    d_kv_pre = jnp.concatenate([d_key_pre.astype(BF), d_kv[:, head_dim:].astype(BF)], axis=1)
    d_normed_one = mm_nt(d_kv_pre, kv_weight)
    for h in range(heads):
        d_normed_one = d_normed_one + mm_nt(d_query_pre[h], all_query[h])
    d_inputs, d_in_gain = in_pull(d_normed_one)
    grad_tokens = d_inputs + d_middle

    grad_query = jnp.einsum("rd,hrk->hdk", normed_one, d_query_pre, preferred_element_type=F32)
    grad_kv = mm_tn(normed_one, d_kv_pre)
    grad_out = lax.psum_scatter(grad_out.astype(BF), "head", scatter_dimension=0, tiled=False)
    grad_query = lax.psum_scatter(grad_query.astype(BF), "head", scatter_dimension=0, tiled=False)
    grad_out, grad_query = lax.psum((grad_out, grad_query), "ctx")
    grad_kv = lax.psum(grad_kv.astype(BF), AXES).astype(F32)
    gains = [d_in_gain, d_post_gain, d_ffn_gain, d_out_gain, d_query_gain, d_key_gain]
    sizes = [g.shape[0] for g in gains]
    flat = lax.psum(jnp.concatenate(gains), AXES)
    pieces, at = [], 0
    for size in sizes:
        pieces.append(flat[at : at + size])
        at += size
    return (
        output.reshape(micro, rows, width),
        grad_tokens.reshape(micro, rows, width),
        pieces[0],
        grad_query.astype(F32),
        grad_kv[:, :head_dim],
        grad_kv[:, head_dim:],
        pieces[4],
        pieces[5],
        grad_out.astype(F32),
        pieces[1],
        pieces[2],
        jnp.stack([grad_gate.astype(F32), grad_up.astype(F32)], axis=1),
        grad_down.astype(F32),
        pieces[3],
    )


def solution(mesh):
    in_specs = (
        P(None, ("ctx", "head"), None),
        P(),
        P(),
        P(None, "head"),
        P(),
        P(),
        P(),
        P(),
        P("head", None),
        P(),
        P(),
        P(None, None, "head"),
        P("head", None),
        P(),
        P(None, ("ctx", "head"), None),
    )
    out_specs = (
        P(None, ("ctx", "head"), None),
        P(None, ("ctx", "head"), None),
        P(),
        P(None, "head"),
        P(),
        P(),
        P(),
        P(),
        P("head", None),
        P(),
        P(),
        P(None, None, "head"),
        P("head", None),
        P(),
    )
    return jax.shard_map(body, mesh=mesh, in_specs=in_specs, out_specs=out_specs, check_vma=False)
```

```python
from functools import partial

import jax
import jax.numpy as jnp
from jax import lax
from jax.experimental import pallas as pl
from jax.experimental.pallas import tpu as pltpu
from jax.sharding import PartitionSpec as P

EPS = 1e-06
THETA = 1000000.0
NEGATIVE = -1e30
AXES = ("ctx", "head")
BF = jnp.bfloat16
F32 = jnp.float32


def rms_norm(field_in, gain_vec):
    return (
        field_in * lax.rsqrt(jnp.mean(field_in * field_in, axis=-1, keepdims=True) + EPS) * gain_vec
    )


def rotate(field_in, cosine, sine_table):
    half_width = field_in.shape[-1] // 2
    first_half = field_in[..., :half_width]
    second_half = field_in[..., half_width:]
    return jnp.concatenate(
        [
            first_half * cosine - second_half * sine_table,
            second_half * cosine + first_half * sine_table,
        ],
        axis=-1,
    )


def prepare(field_in, gain_vec, cosine, sine_table):
    return rotate(rms_norm(field_in, gain_vec), cosine, sine_table)


def gated_gelu(gate_val, up_val):
    return jax.nn.gelu(gate_val, approximate=True) * up_val


def row_starts(lengths_row, token_index):
    seq_ends = jnp.cumsum(lengths_row, dtype=jnp.int32)
    passed = (token_index[:, None] >= seq_ends[None, :]).astype(jnp.int32)
    return jnp.sum(passed * lengths_row[None, :], axis=1, dtype=jnp.int32)


def angles(positions, width):
    half_width = width // 2
    frequency = jnp.power(THETA, -(jnp.arange(half_width, dtype=F32) * 2.0 / width))
    phase_angle = positions.astype(F32)[:, None] * frequency[None, :]
    return (jnp.cos(phase_angle), jnp.sin(phase_angle))


def mm(left, right):
    return jnp.dot(left, right, preferred_element_type=F32)


def mm_nt(left, right):
    return lax.dot_general(left, right, (((1,), (1,)), ((), ())), preferred_element_type=F32)


def mm_tn(left, right):
    return lax.dot_general(left, right, (((0,), (0,)), ((), ())), preferred_element_type=F32)


def block_scalars(meta, seqs, query_ctx, z, z_count, rows):
    first_query = (query_ctx * z_count + z) * rows
    start = jnp.int32(0)
    end = jnp.int32(0)
    for s in range(seqs):
        end = end + meta[s]
        start = jnp.where(first_query >= end, end, start)
    return first_query, start


def scores_of(meta, seqs, q, kv, first_query, first_key, z, rows, head_dim):
    stacked = q.shape[0]
    keys = kv.shape[0]
    scores = mm_nt(q, kv[:, :head_dim]) * (head_dim**-0.5)
    key_row = lax.broadcasted_iota(jnp.int32, (1, keys), 1)
    key_index = first_key + ((key_row // rows) ^ z) * rows + key_row % rows
    query_index = first_query + lax.broadcasted_iota(jnp.int32, (stacked, 1), 0) % rows
    start = jnp.zeros((stacked, 1), jnp.int32)
    end = jnp.int32(0)
    for s in range(seqs):
        end = end + meta[s]
        start = jnp.where(query_index >= end, end, start)
    allowed = (key_index <= query_index) & (key_index >= start)
    return scores, allowed


def forward_kernel(seqs, rows, z_count, meta, q_ref, kv_ref, o_ref, lse_ref, top, total):
    step = pl.program_id(0)
    last = pl.num_programs(0) - 1
    pair, z = meta[seqs], meta[seqs + 1]
    head_dim = q_ref.shape[-1]
    key_ctx = 2 * ((step // 2) ^ pair) + step % 2
    first_key = key_ctx * z_count * rows

    @pl.when(step == 0)
    def _():
        top[...] = jnp.full(top.shape, NEGATIVE, F32)
        total[...] = jnp.zeros(total.shape, F32)
        o_ref[...] = jnp.zeros(o_ref.shape, F32)

    for block in range(2):
        first_query, first_start = block_scalars(meta, seqs, 2 * pair + block, z, z_count, rows)
        needed = (first_key < first_query + rows) & (first_key + z_count * rows > first_start)

        @pl.when(needed)
        def _():
            kv = kv_ref[0]
            scores, allowed = scores_of(
                meta, seqs, q_ref[block], kv, first_query, first_key, z, rows, head_dim
            )
            scores = jnp.where(allowed, scores, NEGATIVE)
            old_top = top[block][:, :1]
            new_top = jnp.maximum(old_top, jnp.max(scores, axis=1, keepdims=True))
            weights = jnp.where(allowed, jnp.exp(scores - new_top), 0.0)
            keep = jnp.exp(old_top - new_top)
            new_total = total[block][:, :1] * keep + jnp.sum(weights, axis=1, keepdims=True)
            o_ref[block] = o_ref[block] * keep + mm(weights.astype(BF), kv[:, head_dim:])
            top[block] = jnp.broadcast_to(new_top, top.shape[1:])
            total[block] = jnp.broadcast_to(new_total, total.shape[1:])

    @pl.when(step == last)
    def _():
        for block in range(2):
            o_ref[block] = o_ref[block] / total[block][:, :1]
            lse_ref[block] = top[block] + jnp.log(total[block])


def backward_kernel(
    seqs, rows, z_count, meta, q_ref, do_ref, o_ref, lse_ref, kv_ref, dq_ref, dkv_ref, delta, acc
):
    step = pl.program_id(0)
    pair, z = meta[seqs], meta[seqs + 1]
    head_dim = q_ref.shape[-1]
    scale = head_dim**-0.5
    key_ctx = 2 * ((step // 2) ^ pair) + step % 2
    first_key = key_ctx * z_count * rows

    @pl.when(step == 0)
    def _():
        dq_ref[...] = jnp.zeros(dq_ref.shape, F32)
        for block in range(2):
            delta[block] = jnp.broadcast_to(
                jnp.sum(o_ref[block] * do_ref[block].astype(F32), axis=1, keepdims=True),
                delta.shape[1:],
            )

    acc[...] = jnp.zeros(acc.shape, F32)
    for block in range(2):
        first_query, first_start = block_scalars(meta, seqs, 2 * pair + block, z, z_count, rows)
        needed = (first_key < first_query + rows) & (first_key + z_count * rows > first_start)

        @pl.when(needed)
        def _():
            kv = kv_ref[0]
            q = q_ref[block]
            d_out = do_ref[block]
            scores, allowed = scores_of(
                meta, seqs, q, kv, first_query, first_key, z, rows, head_dim
            )
            weights = jnp.where(allowed, jnp.exp(scores - lse_ref[block][:, :1]), 0.0)
            d_weights = mm_nt(d_out, kv[:, head_dim:])
            d_scores = (weights * (d_weights - delta[block][:, :1])).astype(BF)
            acc[:, head_dim:] += mm_tn(weights.astype(BF), d_out)
            acc[:, :head_dim] += mm_tn(d_scores, q) * scale
            dq_ref[block] += mm(d_scores, kv[:, :head_dim]) * scale

    dkv_ref[0] = acc[...].astype(BF)


def attend(meta, seqs, rows, z_count, q, kv):
    ctx_count, keys, wide = kv.shape
    _, stacked, head_dim = q.shape
    whole = lambda *shape: pl.BlockSpec(shape, lambda i, m: (0,) * len(shape))
    return pl.pallas_call(
        partial(forward_kernel, seqs, rows, z_count),
        out_shape=(
            jax.ShapeDtypeStruct((2, stacked, head_dim), F32),
            jax.ShapeDtypeStruct((2, stacked, 128), F32),
        ),
        grid_spec=pltpu.PrefetchScalarGridSpec(
            num_scalar_prefetch=1,
            grid=(ctx_count,),
            in_specs=[
                whole(2, stacked, head_dim),
                pl.BlockSpec((1, keys, wide), lambda i, m: (i, 0, 0)),
            ],
            out_specs=(whole(2, stacked, head_dim), whole(2, stacked, 128)),
            scratch_shapes=[pltpu.VMEM((2, stacked, 128), F32)] * 2,
        ),
        compiler_params=pltpu.CompilerParams(
            dimension_semantics=("arbitrary",), vmem_limit_bytes=48 * 2**20
        ),
        name="attend",
    )(meta, q, kv)


def attend_back(meta, seqs, rows, z_count, q, d_out, o, lse, kv):
    ctx_count, keys, wide = kv.shape
    _, stacked, head_dim = q.shape
    whole = lambda *shape: pl.BlockSpec(shape, lambda i, m: (0,) * len(shape))
    return pl.pallas_call(
        partial(backward_kernel, seqs, rows, z_count),
        out_shape=(
            jax.ShapeDtypeStruct((2, stacked, head_dim), F32),
            jax.ShapeDtypeStruct(kv.shape, BF),
        ),
        grid_spec=pltpu.PrefetchScalarGridSpec(
            num_scalar_prefetch=1,
            grid=(ctx_count,),
            in_specs=[
                whole(2, stacked, head_dim),
                whole(2, stacked, head_dim),
                whole(2, stacked, head_dim),
                whole(2, stacked, 128),
                pl.BlockSpec((1, keys, wide), lambda i, m: (i, 0, 0)),
            ],
            out_specs=(
                whole(2, stacked, head_dim),
                pl.BlockSpec((1, keys, wide), lambda i, m: (i, 0, 0)),
            ),
            scratch_shapes=[pltpu.VMEM((2, stacked, 128), F32), pltpu.VMEM((keys, wide), F32)],
        ),
        compiler_params=pltpu.CompilerParams(
            dimension_semantics=("arbitrary",), vmem_limit_bytes=48 * 2**20
        ),
        name="attend_back",
    )(meta, q, d_out, o, lse, kv)


class Exchange:
    def __init__(self, ctx_count, z_count):
        self.ctx_count, self.z_count = ctx_count, z_count
        self.pair_bits = [1 << b for b in range(1, ctx_count.bit_length() - 1)]

    def flip(self, value, ctx_bits, z_bits):
        pairs = [
            (c * self.z_count + z, (c ^ ctx_bits) * self.z_count + (z ^ z_bits))
            for c in range(self.ctx_count)
            for z in range(self.z_count)
        ]
        return lax.ppermute(value, AXES, pairs)

    def core(self, value):
        return self.flip(value, 1, 0)

    def gather(self, even, odd):
        both = jnp.stack([even, odd])
        columns = [both] + [self.flip(both, 0, d) for d in range(1, self.z_count)]
        slots = [[[None] * self.z_count for _ in range(2)] for _ in range(self.ctx_count // 2)]
        for d, column in enumerate(columns):
            for parity, bits in ((0, self.pair_bits), (1, self.pair_bits[::-1])):
                have = {0: column[parity]}
                for bit in bits:
                    order = sorted(have)
                    got = self.flip(jnp.stack([have[s] for s in order]), bit, 0)
                    for position, slot in enumerate(order):
                        have[slot | (bit >> 1)] = got[position]
                for slot, value in have.items():
                    slots[slot][parity][d] = value
        return jnp.stack(
            [jnp.concatenate(line, axis=0) for slot in slots for line in slot], axis=0
        )

    def scatter_sum(self, parts):
        totals = []
        for d in range(self.z_count):
            both = []
            for parity, bits in ((0, self.pair_bits[::-1]), (1, self.pair_bits)):
                have = {s: parts[s, parity, d] for s in range(self.ctx_count // 2)}
                for bit in bits:
                    away = sorted(s for s in have if s & (bit >> 1))
                    got = self.flip(jnp.stack([have[s].astype(BF) for s in away]), bit, 0)
                    for position, slot in enumerate(away):
                        home = slot ^ (bit >> 1)
                        have[home] = have[home].astype(F32) + got[position].astype(F32)
                        del have[slot]
                both.append(have[0])
            both = jnp.stack(both)
            totals.append(both if d == 0 else self.flip(both.astype(BF), 0, d))
        return sum(t.astype(F32) for t in totals)

    def all_sum(self, value, ctx):
        half, width = value.shape[0] // 2, value.shape[1]
        count = self.ctx_count // 2
        piece = half // count
        bit, pair = ctx % 2, ctx // 2
        away = lax.dynamic_slice(value.astype(BF), ((1 - bit) * half, 0), (half, width))
        mine = lax.dynamic_slice(value, (bit * half, 0), (half, width))
        mine = mine + self.core(away).astype(F32)
        low = mine.astype(BF)
        own = lax.dynamic_slice(mine, (pair * piece, 0), (piece, width))
        for s in range(1, count):
            sent = lax.dynamic_slice(low, ((pair ^ s) * piece, 0), (piece, width))
            own = own + self.flip(sent, 2 * s, 0).astype(F32)
        own = own.astype(BF)
        gathered = lax.dynamic_update_slice(jnp.zeros((half, width), BF), own, (pair * piece, 0))
        for s in range(1, count):
            got = self.flip(own, 2 * s, 0)
            gathered = lax.dynamic_update_slice(gathered, got, ((pair ^ s) * piece, 0))
        other = self.core(gathered)
        return jnp.concatenate(
            [jnp.where(bit == 0, gathered, other), jnp.where(bit == 0, other, gathered)]
        )

    def swap(self, value, parity):
        mine = jnp.where(parity == 0, value[0], value[1])
        other = self.core(jnp.where(parity == 0, value[1], value[0]))
        return jnp.where(parity == 0, mine, other), jnp.where(parity == 0, other, mine)


def body(
    tokens,
    lengths,
    attn_in_gain,
    query_weight,
    key_weight,
    value_weight,
    query_gain,
    key_gain,
    out_weight,
    attn_post_gain,
    ffn_in_gain,
    gate_up,
    down_weight,
    ffn_out_gain,
    cotangent,
):
    micro, rows, width = tokens.shape
    seqs = lengths.shape[1]
    head_dim = query_weight.shape[1]
    ffn_local = down_weight.shape[0]
    ctx_count, heads = lax.axis_size("ctx"), lax.axis_size("head")
    ctx, z = lax.axis_index("ctx"), lax.axis_index("head")
    parity, pair = ctx % 2, ctx // 2
    net = Exchange(ctx_count, heads)
    all_rows = micro * rows

    all_query = lax.all_gather(query_weight, "head", axis=0)
    all_out = lax.all_gather(out_weight, "head", axis=0)
    gate_weight, up_weight = gate_up[:, 0, :], gate_up[:, 1, :]
    kv_weight = jnp.concatenate([key_weight, value_weight], axis=1)

    query_index = (ctx * heads + z) * rows + jnp.arange(rows, dtype=jnp.int32)
    tables = [
        angles(query_index - row_starts(lengths[b], query_index), head_dim) for b in range(micro)
    ]
    cosine = jnp.concatenate([t[0] for t in tables])
    sine_table = jnp.concatenate([t[1] for t in tables])
    meta = jnp.concatenate(
        [
            jnp.where(parity == 0, lengths[0], lengths[1]).astype(jnp.int32),
            jnp.stack([pair, z]).astype(jnp.int32),
        ]
    )

    inputs = tokens.astype(F32).reshape(all_rows, width)
    normed_f, in_pull = jax.vjp(rms_norm, inputs, attn_in_gain)
    normed_one = normed_f.astype(BF)
    normed_all = [normed_one] + [net.flip(normed_one, 0, d) for d in range(1, heads)]
    kv_pre = mm(normed_one, kv_weight)
    key_f, key_pull = jax.vjp(
        partial(prepare, cosine=cosine, sine_table=sine_table), kv_pre[:, :head_dim], key_gain
    )
    own_kv = jnp.concatenate([key_f.astype(BF), kv_pre[:, head_dim:].astype(BF)], axis=1)
    even_kv, odd_kv = net.swap(own_kv.reshape(micro, rows, 2 * head_dim), parity)
    kv_slots = net.gather(even_kv, odd_kv)

    query_pre = lax.dot_general(
        normed_one, all_query, (((1,), (1,)), ((), ())), preferred_element_type=F32
    )
    query_pre = jnp.swapaxes(query_pre, 0, 1)
    query_f, query_pull = jax.vjp(
        partial(prepare, cosine=cosine[None], sine_table=sine_table[None]), query_pre, query_gain
    )

    def to_pair(value):
        by_micro = jnp.swapaxes(value.reshape(heads, micro, rows, head_dim), 0, 1)
        even, odd = net.swap(by_micro, parity)
        return jnp.stack([even, odd]).reshape(2, heads * rows, head_dim)

    def from_pair(value):
        first, second = net.swap(value.reshape(2, heads, rows, head_dim), parity)
        return jnp.concatenate([first, second], axis=1)

    queries = to_pair(query_f.astype(BF))
    attended_f, lse = attend(meta, seqs, rows, heads, queries, kv_slots)
    attended = from_pair(attended_f.astype(BF))
    mixed = lax.dot_general(
        jnp.swapaxes(attended, 0, 1).reshape(all_rows, heads * head_dim),
        all_out.reshape(heads * head_dim, width),
        (((1,), (0,)), ((), ())),
        preferred_element_type=F32,
    )
    post_f, post_pull = jax.vjp(rms_norm, mixed, attn_post_gain)
    middle = inputs + post_f
    pre_f, pre_pull = jax.vjp(rms_norm, middle, ffn_in_gain)
    rows_two = [pre_f.astype(BF)]
    rows_two += [net.flip(rows_two[0], 0, d) for d in range(1, heads)]

    branch_parts, hiddens, gelu_pulls = [], [], []
    for d in range(heads):
        hidden_f, gelu_pull = jax.vjp(
            gated_gelu, mm(rows_two[d], gate_weight), mm(rows_two[d], up_weight)
        )
        hiddens.append(hidden_f.astype(BF))
        gelu_pulls.append(gelu_pull)
        part = mm(hiddens[d], down_weight)
        branch_parts.append(part if d == 0 else net.flip(part.astype(BF), 0, d))
    branch = sum(p.astype(F32) for p in branch_parts)
    out_f, out_pull = jax.vjp(rms_norm, branch, ffn_out_gain)
    output = (middle + out_f).astype(BF)

    upstream = cotangent.astype(F32).reshape(all_rows, width)
    d_branch, d_out_gain = out_pull(upstream)
    rows_grad = [d_branch.astype(BF)]
    rows_grad += [net.flip(rows_grad[0], 0, d) for d in range(1, heads)]
    d_gates, d_ups, d_parts = [], [], []
    for d in range(heads):
        d_gate, d_up = gelu_pulls[d](mm_nt(rows_grad[d], down_weight))
        d_gates.append(d_gate.astype(BF))
        d_ups.append(d_up.astype(BF))
        part = mm_nt(d_gates[d], gate_weight) + mm_nt(d_ups[d], up_weight)
        d_parts.append(part if d == 0 else net.flip(part.astype(BF), 0, d))
    d_normed_two = sum(p.astype(F32) for p in d_parts)
    grad_down = mm_tn(jnp.concatenate(hiddens), jnp.concatenate(rows_grad)).astype(BF)
    rows_all = jnp.concatenate(rows_two)
    grad_gate = mm_tn(rows_all, jnp.concatenate(d_gates)).astype(BF)
    grad_up = mm_tn(rows_all, jnp.concatenate(d_ups)).astype(BF)

    d_middle, d_ffn_gain = pre_pull(d_normed_two)
    d_middle = d_middle + upstream
    d_mixed, d_post_gain = post_pull(d_middle)
    d_mixed, grad_down, grad_gate, grad_up = lax.optimization_barrier(
        (d_mixed.astype(BF), grad_down, grad_gate, grad_up)
    )
    grad_down, grad_gate, grad_up = lax.psum((grad_down, grad_gate, grad_up), "ctx")
    out_parts = jnp.einsum("hrk,rd->hkd", attended, d_mixed, preferred_element_type=F32)
    pick = lambda parts, d: lax.dynamic_index_in_dim(parts, z ^ d, 0, keepdims=False)
    grad_out = pick(out_parts, 0)
    for d in range(1, heads):
        grad_out = grad_out + net.flip(pick(out_parts, d).astype(BF), 0, d).astype(F32)
    d_attended = jnp.einsum("rd,hkd->hrk", d_mixed, all_out, preferred_element_type=F32)
    d_attended = to_pair(d_attended.astype(BF))
    d_queries, d_kv_slots = attend_back(
        meta, seqs, rows, heads, queries, d_attended, attended_f, lse, kv_slots
    )
    d_even, d_odd = net.scatter_sum(
        d_kv_slots.reshape(ctx_count // 2, 2, heads, rows, 2 * head_dim)
    )
    first, second = net.swap(jnp.stack([d_even, d_odd]), parity)
    d_kv = jnp.concatenate([first, second])
    d_query_pre, d_query_gain = query_pull(from_pair(d_queries))
    d_key_pre, d_key_gain = key_pull(d_kv[:, :head_dim])
    d_query_pre = d_query_pre.astype(BF)
    d_kv_pre = jnp.concatenate([d_key_pre.astype(BF), d_kv[:, head_dim:].astype(BF)], axis=1)
    d_normed_one = mm_nt(d_kv_pre, kv_weight)
    for h in range(heads):
        d_normed_one = d_normed_one + mm_nt(d_query_pre[h], all_query[h])
    d_inputs, d_in_gain = in_pull(d_normed_one)
    grad_tokens = d_inputs + d_middle

    gains = [d_in_gain, d_post_gain, d_ffn_gain, d_out_gain, d_query_gain, d_key_gain]
    sizes = [g.shape[0] for g in gains]
    sent_width = 3 * head_dim
    gain_rows = 32
    flat = jnp.pad(jnp.concatenate(gains), (0, gain_rows * sent_width - sum(sizes)))
    flat = flat.reshape(gain_rows, sent_width)
    gain_sum = flat
    by_rows = [jnp.concatenate([pick(d_query_pre, 0), d_kv_pre], axis=1)]
    for d in range(1, heads):
        sent = jnp.concatenate([pick(d_query_pre, d), d_kv_pre], axis=1)
        got = net.flip(jnp.concatenate([sent, flat.astype(BF)]), 0, d)
        by_rows.append(got[:all_rows])
        gain_sum = gain_sum + got[all_rows:].astype(F32)
    projected = mm_tn(jnp.concatenate(by_rows), jnp.concatenate(normed_all))
    gain_lines = -(-sum(sizes) // width)
    gain_sum = gain_sum.reshape(-1)[: gain_lines * width].reshape(gain_lines, width)
    used = sent_width + head_dim
    filled = -(-(used + gain_lines) // (16 * ctx_count)) * (16 * ctx_count)
    gain_sum = jnp.pad(gain_sum, ((0, filled - used - gain_lines), (0, 0)))
    sums = net.all_sum(jnp.concatenate([projected, grad_out, gain_sum]), ctx).astype(F32)
    grad_query, grad_kv = sums[:head_dim].T, sums[head_dim:sent_width].T
    grad_out = sums[sent_width:used]
    flat = sums[used : used + gain_lines].reshape(-1)
    pieces, at = [], 0
    for size in sizes:
        pieces.append(flat[at : at + size])
        at += size
    return (
        output.reshape(micro, rows, width),
        grad_tokens.reshape(micro, rows, width),
        pieces[0],
        grad_query,
        grad_kv[:, :head_dim],
        grad_kv[:, head_dim:],
        pieces[4],
        pieces[5],
        grad_out,
        pieces[1],
        pieces[2],
        jnp.stack([grad_gate.astype(F32), grad_up.astype(F32)], axis=1),
        grad_down.astype(F32),
        pieces[3],
    )


def solution(mesh):
    in_specs = (
        P(None, ("ctx", "head"), None),
        P(),
        P(),
        P(None, "head"),
        P(),
        P(),
        P(),
        P(),
        P("head", None),
        P(),
        P(),
        P(None, None, "head"),
        P("head", None),
        P(),
        P(None, ("ctx", "head"), None),
    )
    out_specs = (
        P(None, ("ctx", "head"), None),
        P(None, ("ctx", "head"), None),
        P(),
        P(None, "head"),
        P(),
        P(),
        P(),
        P(),
        P("head", None),
        P(),
        P(),
        P(None, None, "head"),
        P("head", None),
        P(),
    )
    return jax.shard_map(body, mesh=mesh, in_specs=in_specs, out_specs=out_specs, check_vma=False)
```

```python
from functools import partial

import jax
import jax.numpy as jnp
from jax import lax
from jax.experimental import pallas as pl
from jax.experimental.pallas import tpu as pltpu
from jax.sharding import PartitionSpec as P


EPS = 1e-06
THETA = 1000000.0
NEGATIVE = -1e30
AXES = ("ctx", "head")
BF = jnp.bfloat16
MESH = pl.DeviceIdType.MESH
F32 = jnp.float32


def rms_norm(field_in, gain_vec):
    return (
        field_in * lax.rsqrt(jnp.mean(field_in * field_in, axis=-1, keepdims=True) + EPS) * gain_vec
    )


def rotate(field_in, cosine, sine_table):
    half_width = field_in.shape[-1] // 2
    first_half = field_in[..., :half_width]
    second_half = field_in[..., half_width:]
    return jnp.concatenate(
        [
            first_half * cosine - second_half * sine_table,
            second_half * cosine + first_half * sine_table,
        ],
        axis=-1,
    )


def prepare(field_in, gain_vec, cosine, sine_table):
    return rotate(rms_norm(field_in, gain_vec), cosine, sine_table)


def gated_gelu(gate_val, up_val):
    return jax.nn.gelu(gate_val, approximate=True) * up_val


def row_starts(lengths_row, token_index):
    seq_ends = jnp.cumsum(lengths_row, dtype=jnp.int32)
    passed = (token_index[:, None] >= seq_ends[None, :]).astype(jnp.int32)
    return jnp.sum(passed * lengths_row[None, :], axis=1, dtype=jnp.int32)


def angles(positions, width):
    half_width = width // 2
    frequency = jnp.power(THETA, -(jnp.arange(half_width, dtype=F32) * 2.0 / width))
    phase_angle = positions.astype(F32)[:, None] * frequency[None, :]
    return (jnp.cos(phase_angle), jnp.sin(phase_angle))


def mm(left, right):
    return jnp.dot(left, right, preferred_element_type=F32)


def mm_nt(left, right):
    return lax.dot_general(left, right, (((1,), (1,)), ((), ())), preferred_element_type=F32)


def mm_tn(left, right):
    return lax.dot_general(left, right, (((0,), (0,)), ((), ())), preferred_element_type=F32)


def block_scalars(meta, seqs, query_ctx, z, z_count, rows):
    first_query = (query_ctx * z_count + z) * rows
    start = jnp.int32(0)
    end = jnp.int32(0)
    for s in range(seqs):
        end = end + meta[s]
        start = jnp.where(first_query >= end, end, start)
    return first_query, start


def scores_of(meta, seqs, q, kv, first_query, first_key, z, rows, head_dim):
    stacked = q.shape[0]
    keys = kv.shape[0]
    scores = mm_nt(q, kv[:, :head_dim]) * (head_dim**-0.5)
    key_row = lax.broadcasted_iota(jnp.int32, (1, keys), 1)
    key_index = first_key + ((key_row // rows) ^ z) * rows + key_row % rows
    query_index = first_query + lax.broadcasted_iota(jnp.int32, (stacked, 1), 0) % rows
    start = jnp.zeros((stacked, 1), jnp.int32)
    end = jnp.int32(0)
    for s in range(seqs):
        end = end + meta[s]
        start = jnp.where(query_index >= end, end, start)
    allowed = (key_index <= query_index) & (key_index >= start)
    return scores, allowed


def forward_kernel(seqs, rows, z_count, meta, q_ref, kv_ref, o_ref, lse_ref, top, total):
    step = pl.program_id(0)
    last = pl.num_programs(0) - 1
    pair, z = meta[seqs], meta[seqs + 1]
    head_dim = q_ref.shape[-1]
    key_ctx = 2 * ((step // 2) ^ pair) + step % 2
    first_key = key_ctx * z_count * rows

    @pl.when(step == 0)
    def _():
        top[...] = jnp.full(top.shape, NEGATIVE, F32)
        total[...] = jnp.zeros(total.shape, F32)
        o_ref[...] = jnp.zeros(o_ref.shape, F32)

    for block in range(2):
        first_query, first_start = block_scalars(meta, seqs, 2 * pair + block, z, z_count, rows)
        needed = (first_key < first_query + rows) & (first_key + z_count * rows > first_start)

        @pl.when(needed)
        def _():
            kv = kv_ref[0]
            scores, allowed = scores_of(
                meta, seqs, q_ref[block], kv, first_query, first_key, z, rows, head_dim
            )
            scores = jnp.where(allowed, scores, NEGATIVE)
            old_top = top[block][:, :1]
            new_top = jnp.maximum(old_top, jnp.max(scores, axis=1, keepdims=True))
            weights = jnp.where(allowed, jnp.exp(scores - new_top), 0.0)
            keep = jnp.exp(old_top - new_top)
            new_total = total[block][:, :1] * keep + jnp.sum(weights, axis=1, keepdims=True)
            o_ref[block] = o_ref[block] * keep + mm(weights.astype(BF), kv[:, head_dim:])
            top[block] = jnp.broadcast_to(new_top, top.shape[1:])
            total[block] = jnp.broadcast_to(new_total, total.shape[1:])

    @pl.when(step == last)
    def _():
        for block in range(2):
            o_ref[block] = o_ref[block] / total[block][:, :1]
            lse_ref[block] = top[block] + jnp.log(total[block])


def backward_kernel(
    seqs, rows, z_count, meta, q_ref, do_ref, o_ref, lse_ref, kv_ref, dq_ref, dkv_ref, delta, acc
):
    step = pl.program_id(0)
    pair, z = meta[seqs], meta[seqs + 1]
    head_dim = q_ref.shape[-1]
    scale = head_dim**-0.5
    key_ctx = 2 * ((step // 2) ^ pair) + step % 2
    first_key = key_ctx * z_count * rows

    @pl.when(step == 0)
    def _():
        dq_ref[...] = jnp.zeros(dq_ref.shape, F32)
        for block in range(2):
            delta[block] = jnp.broadcast_to(
                jnp.sum(o_ref[block] * do_ref[block].astype(F32), axis=1, keepdims=True),
                delta.shape[1:],
            )

    acc[...] = jnp.zeros(acc.shape, F32)
    for block in range(2):
        first_query, first_start = block_scalars(meta, seqs, 2 * pair + block, z, z_count, rows)
        needed = (first_key < first_query + rows) & (first_key + z_count * rows > first_start)

        @pl.when(needed)
        def _():
            kv = kv_ref[0]
            q = q_ref[block]
            d_out = do_ref[block]
            scores, allowed = scores_of(
                meta, seqs, q, kv, first_query, first_key, z, rows, head_dim
            )
            weights = jnp.where(allowed, jnp.exp(scores - lse_ref[block][:, :1]), 0.0)
            d_weights = mm_nt(d_out, kv[:, head_dim:])
            d_scores = (weights * (d_weights - delta[block][:, :1])).astype(BF)
            acc[:, head_dim:] += mm_tn(weights.astype(BF), d_out)
            acc[:, :head_dim] += mm_tn(d_scores, q) * scale
            dq_ref[block] += mm(d_scores, kv[:, :head_dim]) * scale

    dkv_ref[0] = acc[...].astype(BF)


def attend(meta, seqs, rows, z_count, q, kv):
    ctx_count, keys, wide = kv.shape
    _, stacked, head_dim = q.shape
    whole = lambda *shape: pl.BlockSpec(shape, lambda i, m: (0,) * len(shape))
    return pl.pallas_call(
        partial(forward_kernel, seqs, rows, z_count),
        out_shape=(
            jax.ShapeDtypeStruct((2, stacked, head_dim), F32),
            jax.ShapeDtypeStruct((2, stacked, 128), F32),
        ),
        grid_spec=pltpu.PrefetchScalarGridSpec(
            num_scalar_prefetch=1,
            grid=(ctx_count,),
            in_specs=[
                whole(2, stacked, head_dim),
                pl.BlockSpec((1, keys, wide), lambda i, m: (i, 0, 0)),
            ],
            out_specs=(whole(2, stacked, head_dim), whole(2, stacked, 128)),
            scratch_shapes=[pltpu.VMEM((2, stacked, 128), F32)] * 2,
        ),
        compiler_params=pltpu.CompilerParams(
            dimension_semantics=("arbitrary",), vmem_limit_bytes=48 * 2**20
        ),
        name="attend",
    )(meta, q, kv)


def attend_back(meta, seqs, rows, z_count, q, d_out, o, lse, kv):
    ctx_count, keys, wide = kv.shape
    _, stacked, head_dim = q.shape
    whole = lambda *shape: pl.BlockSpec(shape, lambda i, m: (0,) * len(shape))
    return pl.pallas_call(
        partial(backward_kernel, seqs, rows, z_count),
        out_shape=(
            jax.ShapeDtypeStruct((2, stacked, head_dim), F32),
            jax.ShapeDtypeStruct(kv.shape, BF),
        ),
        grid_spec=pltpu.PrefetchScalarGridSpec(
            num_scalar_prefetch=1,
            grid=(ctx_count,),
            in_specs=[
                whole(2, stacked, head_dim),
                whole(2, stacked, head_dim),
                whole(2, stacked, head_dim),
                whole(2, stacked, 128),
                pl.BlockSpec((1, keys, wide), lambda i, m: (i, 0, 0)),
            ],
            out_specs=(
                whole(2, stacked, head_dim),
                pl.BlockSpec((1, keys, wide), lambda i, m: (i, 0, 0)),
            ),
            scratch_shapes=[pltpu.VMEM((2, stacked, 128), F32), pltpu.VMEM((keys, wide), F32)],
        ),
        compiler_params=pltpu.CompilerParams(
            dimension_semantics=("arbitrary",), vmem_limit_bytes=48 * 2**20
        ),
        name="attend_back",
    )(meta, q, d_out, o, lse, kv)


def partner(ctx, z, ctx_bit, z_flip):
    if ctx_bit:
        ctx = ctx + ctx_bit * (1 - 2 * ((ctx // ctx_bit) % 2))
    bit = 1
    while bit <= z_flip:
        if z_flip & bit:
            z = z + bit * (1 - 2 * ((z // bit) % 2))
        bit *= 2
    return ctx, z


def slot_of(ctx, z, pair_flip, z_flip):
    bit = 1
    while bit <= pair_flip:
        if pair_flip & bit:
            ctx = partner(ctx, z, 2 * bit, 0)[0]
        bit *= 2
    return ctx, partner(ctx, z, 0, z_flip)[1]


def greet(bits, z_count):
    ctx, z = lax.axis_index("ctx"), lax.axis_index("head")
    barrier = pltpu.get_barrier_semaphore()
    others = [partner(ctx, z, bit, 0) for bit in bits]
    others += [partner(ctx, z, 0, d) for d in range(1, z_count)]
    for other in others:
        pl.semaphore_signal(barrier, inc=1, device_id=other, device_id_type=MESH)
    pl.semaphore_wait(barrier, len(others))
    return ctx, z


def gather_kernel(
    bits, z_count, both, query, out, kv_all, query_all, out_all,
    send_kv, recv_kv, send_w, recv_w, send_core, recv_core, local
):
    ctx, z = greet([1] + bits, z_count)
    orders = (bits, bits[::-1])
    sent, placed = [], []

    def send(source, target, send_sem, recv_sem, device):
        copy = pltpu.make_async_remote_copy(
            src_ref=source, dst_ref=target, send_sem=send_sem, recv_sem=recv_sem,
            device_id=device, device_id_type=MESH,
        )
        copy.start()
        sent.append(copy)
        return copy

    weights = ((query, query_all), (out, out_all))

    def kv_source(slot, p, d):
        return both.at[p] if slot == 0 and d == 0 else kv_all.at[slot, p, d]

    def weight_source(w, slot, d):
        if slot == 0 and d == 0:
            return weights[w][0]
        c, zz = slot_of(ctx, z, slot, d)
        return weights[w][1].at[zz, c]

    for p in range(2):
        placed.append(pltpu.make_async_copy(both.at[p], kv_all.at[0, p, 0], local.at[p]))
    for w in range(2):
        placed.append(
            pltpu.make_async_copy(weights[w][0], weights[w][1].at[z, ctx], local.at[2 + w])
        )
    arrived = {}
    for d in range(1, z_count):
        device = partner(ctx, z, 0, d)
        for p in range(2):
            arrived["kv", 0, p, d] = send(
                both.at[p], kv_all.at[0, p, d], send_kv.at[0, p, d], recv_kv.at[0, p, d], device
            )
        for w in range(2):
            arrived["w", 0, w, d] = send(
                weights[w][0], weights[w][1].at[z, ctx],
                send_w.at[0, w, d], recv_w.at[0, w, d], device,
            )
    for copy in placed:
        copy.start()
    crossed = []

    def cross(w, slot, d):
        c, zz = slot_of(ctx, z, slot, d)
        crossed.append(
            send(
                weight_source(w, slot, d), weights[w][1].at[zz, c],
                send_core.at[slot, w, d], recv_core.at[slot, w, d], partner(ctx, z, 1, 0),
            )
        )

    def stage(j, d):
        for p in range(2):
            have = [0]
            for bit in orders[p][:j]:
                have += [s | (bit >> 1) for s in have]
            fresh = [0] if j == 0 else have[len(have) // 2 :]
            for slot in fresh:
                if slot or d:
                    arrived["kv", slot, p, d].wait_recv()
                    arrived["w", slot, p, d].wait_recv()
                cross(p, slot, d)
            if j == len(bits):
                continue
            bit = orders[p][j]
            device = partner(ctx, z, bit, 0)
            for slot in have:
                to = slot | (bit >> 1)
                arrived["kv", to, p, d] = send(
                    kv_source(slot, p, d), kv_all.at[to, p, d],
                    send_kv.at[to, p, d], recv_kv.at[to, p, d], device,
                )
                c, zz = slot_of(ctx, z, slot, d)
                arrived["w", to, p, d] = send(
                    weight_source(p, slot, d), weights[p][1].at[zz, c],
                    send_w.at[to, p, d], recv_w.at[to, p, d], device,
                )

    for step in range(z_count + len(bits)):
        for j in range(len(bits) + 1):
            if 0 <= step - j < z_count:
                stage(j, step - j)
    for copy in crossed:
        copy.wait_recv()
    for copy in sent:
        copy.wait_send()
    for copy in placed:
        copy.wait()


def gather_all(ctx_count, z_count, both, query, out):
    bits = [1 << b for b in range(1, ctx_count.bit_length() - 1)]
    pairs = ctx_count // 2
    anywhere = pl.BlockSpec(memory_space=pl.ANY)
    near = pl.BlockSpec(memory_space=pltpu.VMEM)
    semaphores = [pltpu.SemaphoreType.DMA((pairs, 2, z_count))] * 6
    return pl.pallas_call(
        partial(gather_kernel, bits, z_count),
        out_shape=(
            jax.ShapeDtypeStruct((pairs, 2, z_count) + both.shape[1:], BF),
            jax.ShapeDtypeStruct((z_count, ctx_count) + query.shape, BF),
            jax.ShapeDtypeStruct((z_count, ctx_count) + out.shape, BF),
        ),
        in_specs=[near] * 3,
        out_specs=(anywhere,) * 3,
        scratch_shapes=semaphores + [pltpu.SemaphoreType.DMA((4,))],
        compiler_params=pltpu.CompilerParams(collective_id=0, has_side_effects=True),
        name="gather_all",
    )(both, query, out)


def sum_kernel(bits, z_count, parts, total, *scratch):
    count = len(bits)
    got, held = scratch[:count], scratch[count : 2 * count]
    z_got, send_sem, recv_sem, z_send, z_recv = scratch[2 * count :]
    ctx, z = greet(bits, z_count)
    orders = (bits[::-1], bits)
    sent = []

    def send(source, target, send_sem, recv_sem, device):
        copy = pltpu.make_async_remote_copy(
            src_ref=source, dst_ref=target, send_sem=send_sem, recv_sem=recv_sem,
            device_id=device, device_id_type=MESH,
        )
        copy.start()
        sent.append(copy)
        return copy

    names = []
    for p in range(2):
        have = list(range(2**count))
        names.append([have])
        for bit in orders[p]:
            have = [s for s in have if not s & (bit >> 1)]
            names[p].append(have)
    flying = {}

    def value(j, p, d, slot):
        if j == 0:
            return parts.at[slot, p, d]
        return held[j - 1].at[names[p][j].index(slot), p, d]

    def stage(j, d):
        for p in range(2):
            if j:
                for i, slot in enumerate(names[p][j]):
                    flying[j - 1, p, d, i].wait_recv()
                    mine = value(j - 1, p, d, slot)[...].astype(F32)
                    held[j - 1][i, p, d] = (mine + got[j - 1][i, p, d].astype(F32)).astype(BF)
            if j < count:
                bit = orders[p][j]
                device = partner(ctx, z, bit, 0)
                for i, slot in enumerate(names[p][j + 1]):
                    flying[j, p, d, i] = send(
                        value(j, p, d, slot | (bit >> 1)), got[j].at[i, p, d],
                        send_sem.at[j, i, p, d], recv_sem.at[j, i, p, d], device,
                    )
            elif d:
                flying["z", p, d] = send(
                    value(count, p, d, 0), z_got.at[p, d],
                    z_send.at[p, d], z_recv.at[p, d], partner(ctx, z, 0, d),
                )

    order = list(range(1, z_count)) + [0]
    for step in range(z_count + count):
        for j in range(count + 1):
            if 0 <= step - j < z_count:
                stage(j, order[step - j])
    for p in range(2):
        sums = held[count - 1][0, p, 0].astype(F32)
        for d in range(1, z_count):
            flying["z", p, d].wait_recv()
            sums = sums + z_got[p, d].astype(F32)
        total[p] = sums
    for copy in sent:
        copy.wait_send()


def sum_all(ctx_count, z_count, parts):
    bits = [1 << b for b in range(1, ctx_count.bit_length() - 1)]
    pairs, _, _, rows, wide = parts.shape
    sizes = [pairs >> (j + 1) for j in range(len(bits))]
    buffers = [pltpu.VMEM((n, 2, z_count, rows, wide), BF) for n in sizes]
    near = pl.BlockSpec(memory_space=pltpu.VMEM)
    return pl.pallas_call(
        partial(sum_kernel, bits, z_count),
        out_shape=jax.ShapeDtypeStruct((2, rows, wide), F32),
        in_specs=[near],
        out_specs=near,
        scratch_shapes=buffers
        + buffers
        + [pltpu.VMEM((2, z_count, rows, wide), BF)]
        + [pltpu.SemaphoreType.DMA((len(bits), pairs // 2, 2, z_count))] * 2
        + [pltpu.SemaphoreType.DMA((2, z_count))] * 2,
        compiler_params=pltpu.CompilerParams(
            collective_id=1, has_side_effects=True, vmem_limit_bytes=60 * 2**20
        ),
        name="sum_all",
    )(parts)


class Exchange:
    def __init__(self, ctx_count, z_count):
        self.ctx_count, self.z_count = ctx_count, z_count

    def flip(self, value, ctx_bits, z_bits):
        pairs = [
            (c * self.z_count + z, (c ^ ctx_bits) * self.z_count + (z ^ z_bits))
            for c in range(self.ctx_count)
            for z in range(self.z_count)
        ]
        return lax.ppermute(value, AXES, pairs)

    def core(self, value):
        return self.flip(value, 1, 0)

    def own_piece(self, value, ctx):
        count = self.ctx_count // 2
        bit, pair = ctx % 2, ctx // 2
        by_core = value.reshape((count, 2) + value.shape[1:])
        take = lambda array, i, axis: lax.dynamic_index_in_dim(array, i, axis, keepdims=False)
        away = self.core(take(by_core, 1 - bit, 1))
        mine = (take(by_core, bit, 1).astype(F32) + away.astype(F32)).astype(BF)
        own = take(mine, pair, 0).astype(F32)
        for s in range(1, count):
            got = self.flip(take(mine, pair ^ s, 0), 2 * s, 0)
            own = own + got.astype(F32)
        return own

    def all_pieces(self, own, ctx):
        count = self.ctx_count // 2
        bit, pair = ctx % 2, ctx // 2
        own = own[None]
        gathered = jnp.zeros((count,) + own.shape[1:], own.dtype)
        gathered = lax.dynamic_update_slice(gathered, own, (pair, 0, 0))
        for s in range(1, count):
            got = self.flip(own, 2 * s, 0)
            gathered = lax.dynamic_update_slice(gathered, got, (pair ^ s, 0, 0))
        other = self.core(gathered)
        both = [jnp.where(bit == 0, gathered, other), jnp.where(bit == 0, other, gathered)]
        return jnp.stack(both, axis=1).reshape((2 * count,) + own.shape[1:])

    def swap(self, value, parity):
        mine = jnp.where(parity == 0, value[0], value[1])
        other = self.core(jnp.where(parity == 0, value[1], value[0]))
        return jnp.where(parity == 0, mine, other), jnp.where(parity == 0, other, mine)


def layer(
    tokens,
    lengths,
    attn_in_gain,
    query_weight,
    key_weight,
    value_weight,
    query_gain,
    key_gain,
    out_weight,
    attn_post_gain,
    ffn_in_gain,
    gate_up,
    down_weight,
    ffn_out_gain,
    cotangent,
):
    micro, rows, width = tokens.shape
    seqs = lengths.shape[1]
    head_dim = query_weight.shape[1]
    ctx_count, heads = lax.axis_size("ctx"), lax.axis_size("head")
    ctx, z = lax.axis_index("ctx"), lax.axis_index("head")
    parity, pair = ctx % 2, ctx // 2
    net = Exchange(ctx_count, heads)
    all_rows = micro * rows

    gate_weight, up_weight = gate_up[:, 0, :], gate_up[:, 1, :]
    kv_weight = jnp.concatenate([key_weight, value_weight], axis=1)

    query_index = (ctx * heads + z) * rows + jnp.arange(rows, dtype=jnp.int32)
    tables = [
        angles(query_index - row_starts(lengths[b], query_index), head_dim) for b in range(micro)
    ]
    cosine = jnp.concatenate([t[0] for t in tables])
    sine_table = jnp.concatenate([t[1] for t in tables])
    meta = jnp.concatenate(
        [
            jnp.where(parity == 0, lengths[0], lengths[1]).astype(jnp.int32),
            jnp.stack([pair, z]).astype(jnp.int32),
        ]
    )

    inputs = tokens.astype(F32).reshape(all_rows, width)
    normed_f, in_pull = jax.vjp(rms_norm, inputs, attn_in_gain)
    normed_one = normed_f.astype(BF)
    kv_pre = mm(normed_one, kv_weight)
    key_f, key_pull = jax.vjp(
        partial(prepare, cosine=cosine, sine_table=sine_table), kv_pre[:, :head_dim], key_gain
    )
    own_kv = jnp.concatenate([key_f.astype(BF), kv_pre[:, head_dim:].astype(BF)], axis=1)
    even_kv, odd_kv = net.swap(own_kv.reshape(micro, rows, 2 * head_dim), parity)
    cut = lambda weight: lax.dynamic_slice_in_dim(
        weight, ctx * (weight.shape[0] // ctx_count), weight.shape[0] // ctx_count, 0
    )
    kv_slots, all_query, all_out = gather_all(
        ctx_count, heads, jnp.stack([even_kv, odd_kv]), cut(query_weight), cut(out_weight)
    )
    kv_slots = kv_slots.reshape(ctx_count, heads * rows, 2 * head_dim)
    all_query = all_query.reshape(heads, width, head_dim)
    all_out = all_out.reshape(heads, head_dim, width)

    query_pre = lax.dot_general(
        normed_one, all_query, (((1,), (1,)), ((), ())), preferred_element_type=F32
    )
    query_pre = jnp.swapaxes(query_pre, 0, 1)
    query_f, query_pull = jax.vjp(
        partial(prepare, cosine=cosine[None], sine_table=sine_table[None]), query_pre, query_gain
    )

    def to_pair(value):
        by_micro = jnp.swapaxes(value.reshape(heads, micro, rows, head_dim), 0, 1)
        even, odd = net.swap(by_micro, parity)
        return jnp.stack([even, odd]).reshape(2, heads * rows, head_dim)

    def from_pair(value):
        first, second = net.swap(value.reshape(2, heads, rows, head_dim), parity)
        return jnp.concatenate([first, second], axis=1)

    queries = to_pair(query_f.astype(BF))
    attended_f, lse = attend(meta, seqs, rows, heads, queries, kv_slots)
    attended = from_pair(attended_f.astype(BF))
    mixed = lax.dot_general(
        jnp.swapaxes(attended, 0, 1).reshape(all_rows, heads * head_dim),
        all_out.reshape(heads * head_dim, width),
        (((1,), (0,)), ((), ())),
        preferred_element_type=F32,
    )
    post_f, post_pull = jax.vjp(rms_norm, mixed, attn_post_gain)
    middle = inputs + post_f
    pre_f, pre_pull = jax.vjp(rms_norm, middle, ffn_in_gain)
    rows_two = [pre_f.astype(BF)]
    rows_two += [net.flip(rows_two[0], 0, d) for d in range(1, heads)]

    branch_parts, hiddens, gelu_pulls = [], [], []
    for d in range(heads):
        hidden_f, gelu_pull = jax.vjp(
            gated_gelu, mm(rows_two[d], gate_weight), mm(rows_two[d], up_weight)
        )
        hiddens.append(hidden_f.astype(BF))
        gelu_pulls.append(gelu_pull)
        part = mm(hiddens[d], down_weight)
        branch_parts.append(part if d == 0 else net.flip(part.astype(BF), 0, d))
    branch = sum(p.astype(F32) for p in branch_parts)
    out_f, out_pull = jax.vjp(rms_norm, branch, ffn_out_gain)
    output = (middle + out_f).astype(BF)

    upstream = cotangent.astype(F32).reshape(all_rows, width)
    d_branch, d_out_gain = out_pull(upstream)
    rows_grad = [d_branch.astype(BF)]
    rows_grad += [net.flip(rows_grad[0], 0, d) for d in range(1, heads)]
    d_gates, d_ups, d_parts = [], [], []
    for d in range(heads):
        d_gate, d_up = gelu_pulls[d](mm_nt(rows_grad[d], down_weight))
        d_gates.append(d_gate.astype(BF))
        d_ups.append(d_up.astype(BF))
        part = mm_nt(d_gates[d], gate_weight) + mm_nt(d_ups[d], up_weight)
        d_parts.append(part if d == 0 else net.flip(part.astype(BF), 0, d))
    d_normed_two = sum(p.astype(F32) for p in d_parts)
    grad_down = mm_tn(jnp.concatenate(hiddens), jnp.concatenate(rows_grad)).astype(BF)
    rows_all = jnp.concatenate(rows_two)
    grad_gate = mm_tn(rows_all, jnp.concatenate(d_gates)).astype(BF)
    grad_up = mm_tn(rows_all, jnp.concatenate(d_ups)).astype(BF)

    d_middle, d_ffn_gain = pre_pull(d_normed_two)
    d_middle = d_middle + upstream
    d_mixed, d_post_gain = post_pull(d_middle)
    d_mixed = d_mixed.astype(BF)
    grad_down, grad_gate, grad_up = lax.psum((grad_down, grad_gate, grad_up), "ctx")
    out_parts = jnp.einsum("hrk,rd->hdk", attended, d_mixed, preferred_element_type=F32)
    pick = lambda parts, d: lax.dynamic_index_in_dim(parts, z ^ d, 0, keepdims=False)
    grad_out = pick(out_parts, 0)
    for d in range(1, heads):
        got = net.flip(pick(out_parts, d).astype(BF), 0, d)
        grad_out = grad_out + got.astype(F32)
    d_attended = jnp.einsum("rd,hkd->hrk", d_mixed, all_out, preferred_element_type=F32)
    d_attended = to_pair(d_attended.astype(BF))
    d_queries, d_kv_slots = attend_back(
        meta, seqs, rows, heads, queries, d_attended, attended_f, lse, kv_slots
    )
    d_query_pre, d_query_gain = query_pull(from_pair(d_queries))
    d_query_pre = d_query_pre.astype(BF)
    piece = width // ctx_count
    query_parts = jnp.einsum("rd,hrk->dhk", normed_one, d_query_pre, preferred_element_type=F32)
    query_parts = query_parts.astype(BF).reshape(ctx_count, piece, heads, head_dim)
    query_parts = jnp.swapaxes(query_parts, 1, 2).reshape(ctx_count, heads * piece, head_dim)
    query_parts = net.own_piece(query_parts, ctx)
    query_parts = query_parts.reshape(heads, piece, head_dim)
    d_kv_own = sum_all(
        ctx_count, heads, d_kv_slots.reshape(ctx_count // 2, 2, heads, rows, 2 * head_dim)
    )
    first, second = net.swap(d_kv_own, parity)
    d_kv = jnp.concatenate([first, second])
    d_key_pre, d_key_gain = key_pull(d_kv[:, :head_dim])
    d_kv_pre = jnp.concatenate([d_key_pre.astype(BF), d_kv[:, head_dim:].astype(BF)], axis=1)
    d_normed_one = mm_nt(d_kv_pre, kv_weight)
    for h in range(heads):
        d_normed_one = d_normed_one + mm_nt(d_query_pre[h], all_query[h])
    d_inputs, d_in_gain = in_pull(d_normed_one)
    grad_tokens = d_inputs + d_middle

    gains = [d_in_gain, d_post_gain, d_ffn_gain, d_out_gain, d_query_gain, d_key_gain]
    sizes = [g.shape[0] for g in gains]
    grad_key = mm_tn(normed_one, d_kv_pre[:, :head_dim])
    grad_value = mm_tn(normed_one, d_kv_pre[:, head_dim:])
    gain_rows = -(-sum(sizes) // (16 * ctx_count * head_dim)) * 16
    flat = jnp.concatenate(gains)
    flat = jnp.pad(flat, (0, ctx_count * gain_rows * head_dim - sum(sizes)))
    split = lambda value: value.astype(BF).reshape(ctx_count, -1, head_dim)
    mixed_parts = jnp.concatenate(
        [split(v) for v in (grad_out, grad_key, grad_value, flat)], axis=1
    )
    own = net.own_piece(mixed_parts, ctx)
    shared = own[piece:]
    total = jnp.concatenate([pick(query_parts, 0), shared])
    for d in range(1, heads):
        sent = jnp.concatenate([pick(query_parts, d), shared]).astype(BF)
        total = total + net.flip(sent, 0, d).astype(F32)
    sums = net.all_pieces(jnp.concatenate([total, own[:piece]]).astype(BF), ctx)
    part = lambda first, count: sums[:, first : first + count].astype(F32).reshape(-1, head_dim)
    grad_query, grad_key, grad_value = (part(i * piece, piece) for i in range(3))
    flat = part(3 * piece, gain_rows).reshape(-1)
    grad_out = part(3 * piece + gain_rows, piece)
    pieces, at = [], 0
    for size in sizes:
        pieces.append(flat[at : at + size])
        at += size
    grad_mix = jnp.stack([grad_gate.astype(F32), grad_up.astype(F32)], axis=1)
    grad_down = grad_down.astype(F32)
    return (
        output.reshape(micro, rows, width),
        grad_tokens.reshape(micro, rows, width),
        pieces[0],
        grad_query,
        grad_key,
        grad_value,
        pieces[4],
        pieces[5],
        grad_out.T,
        pieces[1],
        pieces[2],
        grad_mix,
        grad_down,
        pieces[3],
    )


def solution(mesh):
    in_specs = (
        P(None, ("ctx", "head"), None),
        P(),
        P(),
        P(None, "head"),
        P(),
        P(),
        P(),
        P(),
        P("head", None),
        P(),
        P(),
        P(None, None, "head"),
        P("head", None),
        P(),
        P(None, ("ctx", "head"), None),
    )
    out_specs = (
        P(None, ("ctx", "head"), None),
        P(None, ("ctx", "head"), None),
        P(),
        P(None, "head"),
        P(),
        P(),
        P(),
        P(),
        P("head", None),
        P(),
        P(),
        P(None, None, "head"),
        P("head", None),
        P(),
    )
    return jax.shard_map(layer, mesh=mesh, in_specs=in_specs, out_specs=out_specs, check_vma=False)
```
